32 devices in a mesh: seq: 8 (over z, y), head: 4 (over x, core).
Axes of the slice: x: 2, y: 2, z: 4, core: 2. Of those that a mesh axis runs over, the one named last changes fastest.
Arguments:
- queries: bfloat16 [4096, 1024], P('seq', 'head'), may hold values from -6 to 6
- keys: bfloat16 [4096, 1024], P('seq', 'head'), may hold values from -6 to 6
- values: bfloat16 [4096, 1024], P('seq', 'head'), may hold values from -4 to 4
- masked: int32 [4096], P('seq'), may hold values from 0 to 1
- mask_qkv: bfloat16 [3, 1024], P(None, 'head'), may hold values from -5.09375 to 5.09375
- key_bars: int32 [32, 4], P('seq'), may hold values from -1 to 31, as said below
- w_out: bfloat16 [1024, 1536], P('head'), may hold values from -0.1875 to 0.1875
Outputs:
- attn_out: bfloat16 [4096, 1536], P('seq', 'head')
The draws below stay inside these ranges and needn't reach their ends.
Inputs may be any that keep to these rules, and one draw needn't show every extreme that they name: `key_bars`: entry [b, s] is -1 or a bar on the device s - 2 places along seq for s < 2, s - 1 places for s >= 2. Bar b lists bar a in slot s exactly when a lists b in slot 3 - s. No listed bar is b or next to b. The bars of one device list at most 2 bars of any one other device, and some pair of devices reaches 2.
All inputs are finite; a program needn't handle non-finite values.
Results may differ from the reference program's by a relative error of at most 0.009.
Values may be sent and summed in bfloat16 or wider, within the bound.
A program may use at most 64 MiB of HBM per device.

```python
import math
import jax
import jax.numpy as jnp
from jax import lax

D = 1536
HEADS = 16
HD = 64
BAR = 128
R = 2
BARS_DEV = 4
CAP = 2
NBARS = 32
TOKENS = 4096
N_HEAD = 4


def masked_plan(key):
    return (jax.random.randint(jax.random.fold_in(key, 5), (TOKENS,), 0, 3) == 0).astype(jnp.int32)


def draw_masked(key, part):
    return masked_plan(key)


def base_draw(key, salt):
    local_key = jax.random.fold_in(key, salt)
    return jnp.clip(jax.random.normal(jax.random.fold_in(local_key, 1), (TOKENS, HEADS * HD), jnp.float32), -3.0, 3.0) * 1.7


def draw_queries(key, part):
    result = base_draw(key, 31)
    return result.astype(jnp.bfloat16)


def draw_keys(key, part):
    result = base_draw(key, 32)
    return result.astype(jnp.bfloat16)


def draw_key_bars(key, part):
    devices = NBARS // BARS_DEV
    dev_ids = jnp.arange(devices, dtype=jnp.int32)
    levels = jax.random.randint(jax.random.fold_in(key, 11), (devices,), max(CAP // 2, 1), CAP + 1)
    levels = jnp.where(dev_ids <= R, CAP, levels).astype(jnp.int32)
    table = jnp.full((NBARS, 2 * R), -1, jnp.int32)
    local_ids = jnp.arange(BARS_DEV, dtype=jnp.int32)
    for offset in range(1, R + 1):
        pairs = devices - offset
        counts = jnp.minimum(levels[:pairs], levels[offset:])
        offset_key = jax.random.fold_in(key, 20 + offset)
        send_score = jax.random.randint(jax.random.fold_in(offset_key, 1), (pairs, BARS_DEV), 0, 2 ** 20) * BARS_DEV + local_ids[None, :]
        if offset == 1:
            send_score = jnp.where(local_ids[None, :] == BARS_DEV - 1, 2 ** 30, send_score)
        recv_score = jax.random.randint(jax.random.fold_in(offset_key, 2), (pairs, BARS_DEV), 0, 2 ** 20) * BARS_DEV + local_ids[None, :]
        send_order = jnp.argsort(send_score, axis=1, stable=True).astype(jnp.int32)
        recv_order = jnp.argsort(recv_score, axis=1, stable=True).astype(jnp.int32)
        live = local_ids[None, :] < counts[:, None]
        sender = dev_ids[:pairs, None] * BARS_DEV + send_order
        receiver = (dev_ids[:pairs, None] + offset) * BARS_DEV + recv_order
        table = table.at[sender.reshape(-1), R + offset - 1].set(jnp.where(live, receiver, -1).reshape(-1))
        table = table.at[receiver.reshape(-1), R - offset].set(jnp.where(live, sender, -1).reshape(-1))
    return table


def block_levels(own_key, dims, split, low, top_value):
    loudness = 1.0
    for axis_at, blocks in split:
        steps = jax.random.uniform(jax.random.fold_in(jax.random.fold_in(own_key, 6), axis_at), (blocks,), jnp.float32, low / len(split), top_value / len(split))
        loudness = loudness * jnp.repeat(jnp.exp(steps), dims[axis_at] // blocks).reshape((-1,) + (1,) * (len(dims) - 1 - axis_at))
    return loudness


def gaussian(own_key, shape, spread, most, cuts=(), kind=jnp.bfloat16):
    drawn = spread * jax.random.normal(own_key, shape, jnp.float32)
    if cuts:
        drawn = drawn * block_levels(own_key, shape, cuts, -0.22, 0.18)
    return jnp.clip(drawn, -most, most).astype(kind)


def setup_inputs(seed: int = 0) -> dict:
    splits = jax.random.split(jax.random.key(seed), 8)
    return {
        "queries": draw_queries(jax.random.fold_in(splits[7], 71), 0),
        "keys": draw_keys(jax.random.fold_in(splits[7], 71), 0),
        "values": gaussian(splits[2], (TOKENS, HEADS * HD), 1.0, 4.0, ((0, 8), (1, 4))),
        "masked": draw_masked(jax.random.fold_in(splits[7], 71), 0),
        "mask_qkv": gaussian(splits[4], (3, HEADS * HD), 1.7, 5.09375, ((1, 4),)),
        "key_bars": draw_key_bars(jax.random.fold_in(splits[7], 71), 0),
        "w_out": gaussian(splits[6], (HEADS * HD, D), (HEADS * HD) ** -0.5, 0.1875, ((0, 4),)),
    }


def attend_group(query_grp, key_grp, value_grp, usable):
    scaling = 1.0 / math.sqrt(HD)
    scores = jnp.einsum('gqhd,gnkhd->ghqnk', query_grp.astype(jnp.float32), key_grp.astype(jnp.float32)) * scaling
    scores = jnp.where(usable[:, None, None, :, None], scores, -jnp.inf)
    row_max = lax.optimization_barrier(jnp.max(scores, axis=(3, 4), keepdims=True))
    raised = jnp.exp(scores - row_max)
    totals = lax.optimization_barrier(jnp.sum(raised, axis=(3, 4)))
    rounded = lax.optimization_barrier(raised.astype(jnp.bfloat16)).astype(jnp.float32)
    weighted = jnp.einsum('ghqnk,gnkhd->gqhd', rounded, value_grp.astype(jnp.float32))
    return (weighted / jnp.transpose(totals, (0, 2, 1))[..., None]).astype(jnp.bfloat16)

def reference(queries, keys, values, masked, mask_qkv, key_bars, w_out):
    flagged = (masked == 1)[:, None]
    query_eff = jnp.where(flagged, mask_qkv[0][None, :], queries)
    key_eff = jnp.where(flagged, mask_qkv[1][None, :], keys)
    value_eff = jnp.where(flagged, mask_qkv[2][None, :], values)
    shaped = (NBARS, BAR, HEADS, HD)
    query_blocks = query_eff.reshape(shaped)
    key_blocks = key_eff.reshape(shaped)
    value_blocks = value_eff.reshape(shaped)
    bar_ids = jnp.arange(NBARS, dtype=jnp.int32)
    band_ids = jnp.stack([bar_ids - 1, bar_ids, bar_ids + 1], axis=1)
    listed = jnp.concatenate([band_ids, key_bars.astype(jnp.int32)], axis=1).astype(jnp.int32)
    usable = jnp.concatenate([(band_ids >= 0) & (band_ids < NBARS), key_bars >= 0], axis=1)
    listed = jnp.clip(listed, 0, NBARS - 1)
    group_size = 8

    def one_group(start):
        row_ids = start + jnp.arange(group_size, dtype=jnp.int32)
        picked = listed[row_ids]
        return attend_group(query_blocks[row_ids], key_blocks[picked], value_blocks[picked], usable[row_ids])
    starts = jnp.arange(0, NBARS, group_size, dtype=jnp.int32)
    attended = lax.map(one_group, starts).reshape(TOKENS, HEADS * HD)
    head_split = HEADS * HD // N_HEAD
    summed = jnp.zeros((TOKENS, D), jnp.float32)
    for member in range(N_HEAD):
        partial_value = jnp.dot(attended[:, member * head_split:(member + 1) * head_split], w_out[member * head_split:(member + 1) * head_split], preferred_element_type=jnp.float32)
        summed = summed + lax.optimization_barrier(partial_value.astype(jnp.bfloat16)).astype(jnp.float32)
    return summed.astype(jnp.bfloat16)
```

```python
import functools

import jax
import jax.numpy as jnp
from jax import lax
from jax.experimental import pallas as pl
from jax.experimental.pallas import tpu as pltpu
from jax.sharding import PartitionSpec as P

HD = 64
R = 2
CAP = 2
LANES = 128
MESH = pl.DeviceIdType.MESH
NEG = -1e30


def kernel(
    n_seq, n_head, bars_ref, masked_ref, mask_ref, q_ref, k_ref, v_ref, w_ref, out_ref,
    kv, qs, pack, got_a, got_b, got_c, got_d, rim, w_all, att, top, tot, acc,
    halo_send, halo_recv, rim_send, rim_recv, w_send, w_recv, w_own, att_send, att_recv,
):
    seq = lax.axis_index("seq")
    head = lax.axis_index("head")
    bar_count, bar_len, width = q_ref.shape
    tiles = width // LANES
    per_tile = LANES // HD
    out_cols = w_all.shape[2]
    columns = 2 * R
    got = (got_a, got_b, got_c, got_d)
    offsets = [c - R if c < R else c - R + 1 for c in range(columns)]
    low, high = R - 1, R

    def there(offset):
        return jnp.logical_and(seq + offset >= 0, seq + offset < n_seq)

    barrier = pltpu.get_barrier_semaphore()
    count = n_head - 1
    for offset in offsets:
        count = count + there(offset).astype(jnp.int32)

        @pl.when(there(offset))
        def _(offset=offset):
            pl.semaphore_signal(
                barrier, inc=1, device_id=(seq + offset, head), device_id_type=MESH
            )

    peers = [lax.rem(head + step, n_head) for step in range(1, n_head)]
    for peer in peers:
        pl.semaphore_signal(barrier, inc=1, device_id=(seq, peer), device_id_type=MESH)

    own_w = pltpu.make_async_copy(
        w_ref.at[:, pl.ds(pl.multiple_of(head * out_cols, LANES), out_cols)],
        w_all.at[head],
        w_own,
    )
    own_w.start()

    rows = lax.broadcasted_iota(jnp.int32, (bar_len, bar_len), 0)
    cols = lax.broadcasted_iota(jnp.int32, (bar_len, bar_len), 1)

    def flag(b):
        row = masked_ref[b : b + 1, :]
        return jnp.max(jnp.where(rows == cols, row, 0), axis=1, keepdims=True) == 1

    def replaced(value, row, hit):
        return jnp.where(hit, mask_ref[row : row + 1, :].astype(jnp.float32), value.astype(jnp.float32))

    for b in range(bar_count):
        hit = flag(b)
        kv[b, :, :width] = replaced(k_ref[b], 1, hit).astype(jnp.bfloat16)
        kv[b, :, width:] = replaced(v_ref[b], 2, hit).astype(jnp.bfloat16)

    listed = [[bars_ref[b, c] for c in range(columns)] for b in range(bar_count)]
    for c in (low, high, 0, columns - 1) if R == 2 else range(columns):
        before = jnp.int32(0)
        chosen = [jnp.int32(0)] * CAP
        for b in range(bar_count):
            used = (listed[b][c] >= 0).astype(jnp.int32)
            for slot in range(CAP):
                chosen[slot] = chosen[slot] + jnp.where(before == slot, used * b, 0)
            before = before + used
        for slot in range(CAP):
            pack[c, slot] = kv[chosen[slot]]

    pl.semaphore_wait(barrier, count)

    def halo(c):
        return pltpu.make_async_remote_copy(
            src_ref=pack.at[c],
            dst_ref=got[columns - 1 - c],
            send_sem=halo_send.at[c],
            recv_sem=halo_recv.at[columns - 1 - c],
            device_id=(seq + offsets[c], head),
            device_id_type=MESH,
        )

    def edge(side):
        return pltpu.make_async_remote_copy(
            src_ref=kv.at[bar_count - 1 if side else 0],
            dst_ref=rim.at[1 - side],
            send_sem=rim_send.at[side],
            recv_sem=rim_recv.at[1 - side],
            device_id=(seq + (1 if side else -1), head),
            device_id_type=MESH,
        )

    for c in [low, high] + [c for c in range(columns) if c not in (low, high)]:

        @pl.when(there(offsets[c]))
        def _(c=c):
            halo(c).start()
            if c in (low, high):
                edge(c - low).start()

        @pl.when(jnp.logical_not(there(offsets[c])))
        def _(c=c):
            got[c][...] = jnp.zeros(got[c].shape, got[c].dtype)
            if c in (low, high):
                rim[c - low] = jnp.zeros_like(rim[c - low])

    def w_copy(step):
        peer = peers[step]
        return pltpu.make_async_remote_copy(
            src_ref=w_ref.at[:, pl.ds(pl.multiple_of(peer * out_cols, LANES), out_cols)],
            dst_ref=w_all.at[head],
            send_sem=w_send.at[step],
            recv_sem=w_recv.at[step],
            device_id=(seq, peer),
            device_id_type=MESH,
        )

    for step in range(n_head - 1):
        w_copy(step).start()

    lane = lax.broadcasted_iota(jnp.int32, (bar_len, LANES), 1)
    scaling = HD ** -0.5
    for b in range(bar_count):
        query = replaced(q_ref[b], 0, flag(b)) * scaling
        for t in range(tiles):
            part = query[:, t * LANES : (t + 1) * LANES]
            for h in range(per_tile):
                qs[b, t, h * bar_len : (h + 1) * bar_len, :] = jnp.where(
                    lane // HD == h, part, 0.0
                ).astype(jnp.bfloat16)

    def update(b, t, blocks, first=False, last=False):
        k_at = slice(t * LANES, (t + 1) * LANES)
        v_at = slice(width + t * LANES, width + (t + 1) * LANES)
        query = qs[b, t]
        scores = []
        for ref, index, usable in blocks:
            s = lax.dot_general(
                query, ref[index + (slice(None), k_at)], (((1,), (1,)), ((), ())),
                preferred_element_type=jnp.float32,
            )
            if usable is not None:
                s = s + jnp.where(usable, 0.0, NEG).astype(jnp.float32)
            scores.append(s)
        wide = functools.reduce(jnp.maximum, scores)
        peak = jnp.max(wide, axis=1, keepdims=True)
        if not first:
            old = top[b, t][:, :1]
            peak = jnp.maximum(peak, old)
            fade = jnp.exp(old - peak)
        raised = [jnp.exp(s - peak) for s in scores]
        total = jnp.sum(functools.reduce(jnp.add, raised), axis=1, keepdims=True)
        rounded = jnp.concatenate([r.astype(jnp.bfloat16) for r in raised], axis=1)
        value = jnp.concatenate([ref[index + (slice(None), v_at)] for ref, index, _ in blocks], axis=0)
        weighted = jnp.dot(rounded, value, preferred_element_type=jnp.float32)
        if not first:
            total = total + tot[b, t][:, :1] * fade
            weighted = weighted + acc[b, t] * fade
        if not last:
            top[b, t] = jnp.broadcast_to(peak, top.shape[2:])
            tot[b, t] = jnp.broadcast_to(total, tot.shape[2:])
            acc[b, t] = weighted
            return None
        done = weighted / total
        result = done[:bar_len]
        for h in range(1, per_tile):
            result = jnp.where(lane // HD == h, done[h * bar_len : (h + 1) * bar_len], result)
        return result.astype(jnp.bfloat16)

    for b in range(bar_count):
        blocks = [(kv, (n,), None) for n in range(max(b - 1, 0), min(b + 2, bar_count))]
        for t in range(tiles):
            update(b, t, blocks, first=True)

    def listed_block(b, c):
        wanted = listed[b][c]
        slot = jnp.int32(0)
        for other in range(bar_count):
            held = listed[other][c]
            slot = slot + jnp.logical_and(held >= 0, held < wanted).astype(jnp.int32)
        return (got[c], (jnp.minimum(slot, CAP - 1),), wanted >= 0)

    far = [c for c in range(columns) if c not in (low, high)]
    for c in far:

        @pl.when(there(offsets[c]))
        def _(c=c):
            halo(columns - 1 - c).wait_recv()

    for b in range(bar_count):
        for t in range(tiles):
            update(b, t, [listed_block(b, c) for c in far])

    for c in (low, high):

        @pl.when(there(offsets[c]))
        def _(c=c):
            halo(columns - 1 - c).wait_recv()
            edge(high - c).wait_recv()

    twin = head + 1 - 2 * lax.rem(head, 2)
    across = lax.rem(head + 2, n_head)

    def att_copy(b, kind):
        slot = across if kind == 2 else head
        return pltpu.make_async_remote_copy(
            src_ref=att.at[slot, b],
            dst_ref=att.at[slot, b],
            send_sem=att_send.at[b, kind],
            recv_sem=att_recv.at[b, kind],
            device_id=(seq, across if kind == 1 else twin),
            device_id_type=MESH,
        )

    def relay(b):
        att_copy(b, 1).wait_recv()
        att_copy(b, 2).start()

    order = [0, bar_count - 1] + list(range(1, bar_count - 1))
    for place, b in enumerate(order):
        blocks = [listed_block(b, c) for c in (low, high)]
        if b == 0:
            blocks.append((rim, (0,), there(-1)))
        if b == bar_count - 1:
            blocks.append((rim, (1,), there(1)))
        for t in range(tiles):
            att[head, b, :, t * LANES : (t + 1) * LANES] = update(b, t, blocks, last=True)
        att_copy(b, 1).start()
        att_copy(b, 0).start()
        if place > 1:
            relay(order[place - 2])
    own_w.wait()
    for step in range(n_head - 1):
        w_copy(step).wait_recv()

    def project(b):
        att_copy(b, 0).wait_recv()
        att_copy(b, 2).wait_recv()
        summed = None
        for member in range(n_head):
            term = jnp.dot(att[member, b], w_all[member], preferred_element_type=jnp.float32)
            term = term.astype(jnp.bfloat16).astype(jnp.float32)
            summed = term if summed is None else summed + term
        out_ref[b] = summed.astype(jnp.bfloat16)

    for place, b in enumerate(order):
        if place >= len(order) - 2:
            pass
        elif place + 2 < len(order):
            relay(order[place + 2])
        project(b)

    for c in range(columns):

        @pl.when(there(offsets[c]))
        def _(c=c):
            halo(c).wait_send()
            if c in (low, high):
                edge(c - low).wait_send()

    for step in range(n_head - 1):
        w_copy(step).wait_send()
    for b in range(bar_count):
        for kind in range(3):
            att_copy(b, kind).wait_send()


def solution(mesh):
    n_seq, n_head = mesh.shape["seq"], mesh.shape["head"]

    def on_device(queries, keys, values, masked, mask_qkv, key_bars, w_out):
        tokens, width = queries.shape
        bars = key_bars.shape[0]
        length = tokens // bars
        cols = w_out.shape[1] // n_head
        tiles, rows = width // LANES, LANES // HD * length
        shaped = [x.reshape(bars, length, width) for x in (queries, keys, values)]
        vmem = pl.BlockSpec(memory_space=pltpu.VMEM)
        dma = pltpu.SemaphoreType.DMA
        out = pl.pallas_call(
            functools.partial(kernel, n_seq, n_head),
            out_shape=jax.ShapeDtypeStruct((bars, length, cols), jnp.bfloat16),
            in_specs=[pl.BlockSpec(memory_space=pltpu.SMEM)] + [vmem] * 6,
            out_specs=vmem,
            scratch_shapes=[
                pltpu.VMEM((bars, length, 2 * width), jnp.bfloat16),
                pltpu.VMEM((bars, tiles, rows, LANES), jnp.bfloat16),
                pltpu.VMEM((2 * R, CAP, length, 2 * width), jnp.bfloat16),
            ]
            + [pltpu.VMEM((CAP, length, 2 * width), jnp.bfloat16)] * (2 * R)
            + [
                pltpu.VMEM((2, length, 2 * width), jnp.bfloat16),
                pltpu.VMEM((n_head, width, cols), jnp.bfloat16),
                pltpu.VMEM((n_head, bars, length, width), jnp.bfloat16),
                pltpu.VMEM((bars, tiles, rows, LANES), jnp.float32),
                pltpu.VMEM((bars, tiles, rows, LANES), jnp.float32),
                pltpu.VMEM((bars, tiles, rows, LANES), jnp.float32),
                dma((2 * R,)),
                dma((2 * R,)),
                dma((2,)),
                dma((2,)),
                dma((n_head - 1,)),
                dma((n_head - 1,)),
                dma,
                dma((bars, 3)),
                dma((bars, 3)),
            ],
            compiler_params=pltpu.CompilerParams(
                collective_id=0, has_side_effects=True, vmem_limit_bytes=48 * 1024 * 1024
            ),
            name="bar_attention",
        )(key_bars, masked.reshape(bars, length), mask_qkv, *shaped, w_out)
        return out.reshape(tokens, cols)

    placed = (
        P("seq", "head"),
        P("seq", "head"),
        P("seq", "head"),
        P("seq"),
        P(None, "head"),
        P("seq", None),
        P("head", None),
    )
    return jax.shard_map(
        on_device, mesh=mesh, in_specs=placed, out_specs=P("seq", "head"), check_vma=False
    )
```

```python
import functools

import jax
import jax.numpy as jnp
from jax import lax
from jax.experimental import pallas as pl
from jax.experimental.pallas import tpu as pltpu
from jax.sharding import PartitionSpec as P

HD = 64
R = 2
CAP = 2
CHUNK = 2
LANES = 128
MESH = pl.DeviceIdType.MESH
NEG = -1e30


def kernel(
    n_seq, n_head, bars_ref, masked_ref, mask_ref, q_hbm, k_hbm, v_hbm, w_ref, out_ref,
    q_ref, k_ref, v_ref, in_sem,    kv, qs, pack, got_refs, rim, w_all, att, top, tot, acc,
    halo_send, halo_recv, rim_send, rim_recv, w_send, w_recv, w_own, att_send, att_recv,
):
    seq = lax.axis_index("seq")
    head = lax.axis_index("head")
    bar_count, bar_len, width = q_ref.shape
    tiles = width // LANES
    per_tile = LANES // HD
    out_cols = w_all.shape[2]
    columns = 2 * R
    got = [got_refs[c * tiles : (c + 1) * tiles] for c in range(columns)]
    offsets = [c - R if c < R else c - R + 1 for c in range(columns)]
    low, high = R - 1, R

    def there(offset):
        return jnp.logical_and(seq + offset >= 0, seq + offset < n_seq)

    barrier = pltpu.get_barrier_semaphore()
    count = n_head - 1
    for offset in offsets:
        count = count + there(offset).astype(jnp.int32)

        @pl.when(there(offset))
        def _(offset=offset):
            pl.semaphore_signal(
                barrier, inc=1, device_id=(seq + offset, head), device_id_type=MESH
            )

    peers = [lax.rem(head + step, n_head) for step in range(1, n_head)]
    for peer in peers:
        pl.semaphore_signal(barrier, inc=1, device_id=(seq, peer), device_id_type=MESH)

    loads = [
        pltpu.make_async_copy(source, target, in_sem.at[n])
        for n, (source, target) in enumerate(((k_hbm, k_ref), (v_hbm, v_ref), (q_hbm, q_ref)))
    ]
    for load in loads:
        load.start()
    own_w = pltpu.make_async_copy(
        w_ref.at[:, pl.ds(pl.multiple_of(head * out_cols, LANES), out_cols)],
        w_all.at[head],
        w_own,
    )
    own_w.start()

    rows = lax.broadcasted_iota(jnp.int32, (bar_len, bar_len), 0)
    cols = lax.broadcasted_iota(jnp.int32, (bar_len, bar_len), 1)

    def flag(b):
        row = masked_ref[b : b + 1, :]
        return jnp.max(jnp.where(rows == cols, row, 0), axis=1, keepdims=True) == 1

    def replaced(value, row, hit):
        return jnp.where(hit, mask_ref[row : row + 1, :].astype(jnp.float32), value.astype(jnp.float32))

    loads[0].wait()
    loads[1].wait()
    for b in range(bar_count):
        hit = flag(b)
        key_eff = replaced(k_ref[b], 1, hit).astype(jnp.bfloat16)
        value_eff = replaced(v_ref[b], 2, hit).astype(jnp.bfloat16)
        for t in range(tiles):
            kv[t, b, :, :LANES] = key_eff[:, t * LANES : (t + 1) * LANES]
            kv[t, b, :, LANES:] = value_eff[:, t * LANES : (t + 1) * LANES]

    listed = [[bars_ref[b, c] for c in range(columns)] for b in range(bar_count)]
    for c in (low, high, 0, columns - 1) if R == 2 else range(columns):
        before = jnp.int32(0)
        chosen = [jnp.int32(0)] * CAP
        for b in range(bar_count):
            used = (listed[b][c] >= 0).astype(jnp.int32)
            for slot in range(CAP):
                chosen[slot] = chosen[slot] + jnp.where(before == slot, used * b, 0)
            before = before + used
        for slot in range(CAP):
            for t in range(tiles):
                pack[c, t, slot] = kv[t, chosen[slot]]

    pl.semaphore_wait(barrier, count)

    def halo(c, t):
        return pltpu.make_async_remote_copy(
            src_ref=pack.at[c, t],
            dst_ref=got[columns - 1 - c][t],
            send_sem=halo_send.at[c, t],
            recv_sem=halo_recv.at[columns - 1 - c, t],
            device_id=(seq + offsets[c], head),
            device_id_type=MESH,
        )

    def edge(side, t):
        return pltpu.make_async_remote_copy(
            src_ref=kv.at[t, bar_count - 1 if side else 0],
            dst_ref=rim.at[1 - side, t],
            send_sem=rim_send.at[side, t],
            recv_sem=rim_recv.at[1 - side, t],
            device_id=(seq + (1 if side else -1), head),
            device_id_type=MESH,
        )

    far = [c for c in range(columns) if c not in (low, high)]
    for t in range(tiles):
        for c in [low, high] + far:

            @pl.when(there(offsets[c]))
            def _(c=c, t=t):
                if c in (low, high):
                    edge(c - low, t).start()
                halo(c, t).start()

            @pl.when(jnp.logical_not(there(offsets[c])))
            def _(c=c, t=t):
                got[c][t][...] = jnp.zeros(got[c][t].shape, got[c][t].dtype)
                if c in (low, high):
                    rim[c - low, t] = jnp.zeros(rim.shape[2:], rim.dtype)

    def w_copy(step):
        peer = peers[step]
        return pltpu.make_async_remote_copy(
            src_ref=w_ref.at[:, pl.ds(pl.multiple_of(peer * out_cols, LANES), out_cols)],
            dst_ref=w_all.at[head],
            send_sem=w_send.at[step],
            recv_sem=w_recv.at[step],
            device_id=(seq, peer),
            device_id_type=MESH,
        )

    for step in range(n_head - 1):
        w_copy(step).start()

    lane = lax.broadcasted_iota(jnp.int32, (bar_len, LANES), 1)
    scaling = HD ** -0.5
    loads[2].wait()
    for b in range(bar_count):
        query = replaced(q_ref[b], 0, flag(b)) * scaling
        for t in range(tiles):
            part = query[:, t * LANES : (t + 1) * LANES]
            for h in range(per_tile):
                qs[b, t, h * bar_len : (h + 1) * bar_len, :] = jnp.where(
                    lane // HD == h, part, 0.0
                ).astype(jnp.bfloat16)

    def update(b, t, blocks, first=False, last=False):
        k_at, v_at = slice(0, LANES), slice(LANES, 2 * LANES)
        query = qs[b, t]
        scores = []
        for ref, index, usable in blocks:
            s = lax.dot_general(
                query, ref[index + (slice(None), k_at)], (((1,), (1,)), ((), ())),
                preferred_element_type=jnp.float32,
            )
            if usable is not None:
                s = s + jnp.where(usable, 0.0, NEG).astype(jnp.float32)
            scores.append(s)
        wide = functools.reduce(jnp.maximum, scores)
        peak = jnp.max(wide, axis=1, keepdims=True)
        if not first:
            old = top[b, t][:, :1]
            peak = jnp.maximum(peak, old)
            fade = jnp.exp(old - peak)
        raised = [jnp.exp(s - peak) for s in scores]
        total = jnp.sum(functools.reduce(jnp.add, raised), axis=1, keepdims=True)
        rounded = jnp.concatenate([r.astype(jnp.bfloat16) for r in raised], axis=1)
        value = jnp.concatenate([ref[index + (slice(None), v_at)] for ref, index, _ in blocks], axis=0)
        weighted = jnp.dot(rounded, value, preferred_element_type=jnp.float32)
        if not first:
            total = total + tot[b, t][:, :1] * fade
            weighted = weighted + acc[b, t] * fade
        if not last:
            top[b, t] = jnp.broadcast_to(peak, top.shape[2:])
            tot[b, t] = jnp.broadcast_to(total, tot.shape[2:])
            acc[b, t] = weighted
            return None
        done = weighted / total
        result = done[:bar_len]
        for h in range(1, per_tile):
            result = jnp.where(lane // HD == h, done[h * bar_len : (h + 1) * bar_len], result)
        return result.astype(jnp.bfloat16)

    for t in range(tiles):
        for b in range(bar_count):
            blocks = [(kv, (t, n), None) for n in range(max(b - 1, 0), min(b + 2, bar_count))]
            update(b, t, blocks, first=True)

    def listed_block(b, c, t):
        wanted = listed[b][c]
        slot = jnp.int32(0)
        for other in range(bar_count):
            held = listed[other][c]
            slot = slot + jnp.logical_and(held >= 0, held < wanted).astype(jnp.int32)
        return (got[c][t], (jnp.minimum(slot, CAP - 1),), wanted >= 0)

    twin = head + 1 - 2 * lax.rem(head, 2)
    across = lax.rem(head + 2, n_head)
    chunks = bar_count // CHUNK

    def att_copy(t, g, kind):
        slot = across if kind == 2 else head
        part = att.at[slot, t, g * CHUNK : (g + 1) * CHUNK]
        return pltpu.make_async_remote_copy(
            src_ref=part,
            dst_ref=part,
            send_sem=att_send.at[t, g, kind],
            recv_sem=att_recv.at[t, g, kind],
            device_id=(seq, across if kind == 1 else twin),
            device_id_type=MESH,
        )

    def relay(t, g):
        att_copy(t, g, 1).wait_recv()
        att_copy(t, g, 2).start()

    for t in range(tiles):
        for c in far:

            @pl.when(there(offsets[c]))
            def _(c=c, t=t):
                halo(columns - 1 - c, t).wait_recv()

        for b in range(bar_count):
            update(b, t, [listed_block(b, c, t) for c in far])
        if t > 0:
            for g in range(chunks):
                relay(t - 1, g)
        for c in (low, high):

            @pl.when(there(offsets[c]))
            def _(c=c, t=t):
                halo(columns - 1 - c, t).wait_recv()
                edge(high - c, t).wait_recv()

        for g in range(chunks):
            for b in range(g * CHUNK, (g + 1) * CHUNK):
                blocks = [listed_block(b, c, t) for c in (low, high)]
                if b == 0:
                    blocks.append((rim, (0, t), there(-1)))
                if b == bar_count - 1:
                    blocks.append((rim, (1, t), there(1)))
                att[head, t, b] = update(b, t, blocks, last=True)
            att_copy(t, g, 1).start()
            att_copy(t, g, 0).start()

    own_w.wait()
    for step in range(n_head - 1):
        w_copy(step).wait_recv()
    for g in range(chunks):
        relay(tiles - 1, g)
    for g in range(chunks):
        for t in range(tiles):
            att_copy(t, g, 0).wait_recv()
            att_copy(t, g, 2).wait_recv()
        for b in range(g * CHUNK, (g + 1) * CHUNK):
            summed = None
            for member in range(n_head):
                lhs = jnp.concatenate([att[member, t, b] for t in range(tiles)], axis=1)
                term = jnp.dot(lhs, w_all[member], preferred_element_type=jnp.float32)
                term = term.astype(jnp.bfloat16).astype(jnp.float32)
                summed = term if summed is None else summed + term
            out_ref[b] = summed.astype(jnp.bfloat16)

    for t in range(tiles):
        for c in range(columns):

            @pl.when(there(offsets[c]))
            def _(c=c, t=t):
                halo(c, t).wait_send()
                if c in (low, high):
                    edge(c - low, t).wait_send()

        for g in range(chunks):
            for kind in range(3):
                att_copy(t, g, kind).wait_send()
    for step in range(n_head - 1):
        w_copy(step).wait_send()


def solution(mesh):
    n_seq, n_head = mesh.shape["seq"], mesh.shape["head"]

    def on_device(queries, keys, values, masked, mask_qkv, key_bars, w_out):
        tokens, width = queries.shape
        bars = key_bars.shape[0]
        length = tokens // bars
        cols = w_out.shape[1] // n_head
        tiles, rows = width // LANES, LANES // HD * length
        shaped = [x.reshape(bars, length, width) for x in (queries, keys, values)]
        vmem = pl.BlockSpec(memory_space=pltpu.VMEM)
        dma = pltpu.SemaphoreType.DMA
        out = pl.pallas_call(
            functools.partial(kernel, n_seq, n_head),
            out_shape=jax.ShapeDtypeStruct((bars, length, cols), jnp.bfloat16),
            in_specs=[pl.BlockSpec(memory_space=pltpu.SMEM)] + [vmem] * 2 + [pl.BlockSpec(memory_space=pl.ANY)] * 4,
            out_specs=vmem,
            scratch_shapes=[pltpu.VMEM((bars, length, width), jnp.bfloat16)] * 3
            + [
                dma((3,)),
                pltpu.VMEM((tiles, bars, length, 2 * LANES), jnp.bfloat16),
                pltpu.VMEM((bars, tiles, rows, LANES), jnp.bfloat16),
                pltpu.VMEM((2 * R, tiles, CAP, length, 2 * LANES), jnp.bfloat16),
                [pltpu.VMEM((CAP, length, 2 * LANES), jnp.bfloat16)] * (2 * R * tiles),
                pltpu.VMEM((2, tiles, length, 2 * LANES), jnp.bfloat16),
                pltpu.VMEM((n_head, width, cols), jnp.bfloat16),
                pltpu.VMEM((n_head, tiles, bars, length, LANES), jnp.bfloat16),
                pltpu.VMEM((bars, tiles, rows, LANES), jnp.float32),
                pltpu.VMEM((bars, tiles, rows, LANES), jnp.float32),
                pltpu.VMEM((bars, tiles, rows, LANES), jnp.float32),
                dma((2 * R, tiles)),
                dma((2 * R, tiles)),
                dma((2, tiles)),
                dma((2, tiles)),
                dma((n_head - 1,)),
                dma((n_head - 1,)),
                dma,
                dma((tiles, bars // CHUNK, 3)),
                dma((tiles, bars // CHUNK, 3)),
            ],
            compiler_params=pltpu.CompilerParams(
                collective_id=0, has_side_effects=True
            ),
            name="bar_attention",
        )(key_bars, masked.reshape(bars, length), mask_qkv, *shaped, w_out)
        return out.reshape(tokens, cols)

    placed = (
        P("seq", "head"),
        P("seq", "head"),
        P("seq", "head"),
        P("seq"),
        P(None, "head"),
        P("seq", None),
        P("head", None),
    )
    return jax.shard_map(
        on_device, mesh=mesh, in_specs=placed, out_specs=P("seq", "head"), check_vma=False
    )
```

```python
import functools

import jax
import jax.numpy as jnp
from jax import lax
from jax.experimental import pallas as pl
from jax.experimental.pallas import tpu as pltpu
from jax.sharding import PartitionSpec as P

HD = 64
R = 2
CAP = 2
CHUNK = 1
LANES = 128
MESH = pl.DeviceIdType.MESH
NEG = -1e30


def kernel(
    n_seq, n_head, bars_ref, masked_ref, mask_ref, q_hbm, k_hbm, v_hbm, w_ref, out_ref,
    q_ref, k_ref, v_ref, in_sem,    kv, qs, pack, got_refs, rim, w_all, att, top, tot, acc,
    halo_send, halo_recv, rim_send, rim_recv, w_send, w_recv, w_own, att_send, att_recv,
):
    seq = lax.axis_index("seq")
    head = lax.axis_index("head")
    bar_count, bar_len, width = q_ref.shape
    tiles = width // LANES
    per_tile = LANES // HD
    out_cols = w_all.shape[2]
    columns = 2 * R
    got = [got_refs[c * tiles : (c + 1) * tiles] for c in range(columns)]
    offsets = [c - R if c < R else c - R + 1 for c in range(columns)]
    low, high = R - 1, R

    def there(offset):
        return jnp.logical_and(seq + offset >= 0, seq + offset < n_seq)

    barrier = pltpu.get_barrier_semaphore()
    count = n_head - 1
    for offset in offsets:
        count = count + there(offset).astype(jnp.int32)

        @pl.when(there(offset))
        def _(offset=offset):
            pl.semaphore_signal(
                barrier, inc=1, device_id=(seq + offset, head), device_id_type=MESH
            )

    peers = [lax.rem(head + step, n_head) for step in range(1, n_head)]
    for peer in peers:
        pl.semaphore_signal(barrier, inc=1, device_id=(seq, peer), device_id_type=MESH)

    bar_order = [bar_count - 1, 0] + list(range(1, bar_count - 1))
    loads = {}
    for n, (source, target) in enumerate(((k_hbm, k_ref), (v_hbm, v_ref))):
        for b in range(bar_count):
            loads[n, b] = pltpu.make_async_copy(source.at[b], target.at[b], in_sem.at[n, b])
    for b in bar_order:
        loads[0, b].start()
        loads[1, b].start()
    q_load = pltpu.make_async_copy(q_hbm, q_ref, in_sem.at[2, 0])
    q_load.start()
    own_w = pltpu.make_async_copy(
        w_ref.at[:, pl.ds(pl.multiple_of(head * out_cols, LANES), out_cols)],
        w_all.at[head],
        w_own,
    )
    own_w.start()

    rows = lax.broadcasted_iota(jnp.int32, (bar_len, bar_len), 0)
    cols = lax.broadcasted_iota(jnp.int32, (bar_len, bar_len), 1)

    def flag(b):
        row = masked_ref[b : b + 1, :]
        return jnp.max(jnp.where(rows == cols, row, 0), axis=1, keepdims=True) == 1

    def replaced(value, row, hit):
        return jnp.where(hit, mask_ref[row : row + 1, :].astype(jnp.float32), value.astype(jnp.float32))

    def prepare(b):
        loads[0, b].wait()
        loads[1, b].wait()
        hit = flag(b)
        key_eff = replaced(k_ref[b], 1, hit).astype(jnp.bfloat16)
        value_eff = replaced(v_ref[b], 2, hit).astype(jnp.bfloat16)
        for t in range(tiles):
            kv[t, b, :, :LANES] = key_eff[:, t * LANES : (t + 1) * LANES]
            kv[t, b, :, LANES:] = value_eff[:, t * LANES : (t + 1) * LANES]

    for b in bar_order[:2]:
        prepare(b)

    listed = [[bars_ref[b, c] for c in range(columns)] for b in range(bar_count)]
    picks = []
    for c in range(columns):
        before = jnp.int32(0)
        chosen = [jnp.int32(0)] * CAP
        for b in range(bar_count):
            used = (listed[b][c] >= 0).astype(jnp.int32)
            for slot in range(CAP):
                chosen[slot] = chosen[slot] + jnp.where(before == slot, used * b, 0)
            before = before + used
        picks.append(chosen)

    pl.semaphore_wait(barrier, count)

    def halo(c, t):
        return pltpu.make_async_remote_copy(
            src_ref=pack.at[c, t],
            dst_ref=got[columns - 1 - c][t],
            send_sem=halo_send.at[c, t],
            recv_sem=halo_recv.at[columns - 1 - c, t],
            device_id=(seq + offsets[c], head),
            device_id_type=MESH,
        )

    def edge(side, t):
        return pltpu.make_async_remote_copy(
            src_ref=kv.at[t, bar_count - 1 if side else 0],
            dst_ref=rim.at[1 - side, t],
            send_sem=rim_send.at[side, t],
            recv_sem=rim_recv.at[1 - side, t],
            device_id=(seq + (1 if side else -1), head),
            device_id_type=MESH,
        )

    far = [c for c in range(columns) if c not in (low, high)]
    for c in (low, high):

        @pl.when(there(offsets[c]))
        def _(c=c):
            edge(c - low, 0).start()

    for b in bar_order[2:]:
        prepare(b)
    for t in range(tiles):
        for c in far + [low, high]:
            for slot in range(CAP):
                pack[c, t, slot] = kv[t, picks[c][slot]]

            @pl.when(there(offsets[c]))
            def _(c=c, t=t):
                if c in (low, high) and t > 0:
                    edge(c - low, t).start()
                halo(c, t).start()

            @pl.when(jnp.logical_not(there(offsets[c])))
            def _(c=c, t=t):
                got[c][t][...] = jnp.zeros(got[c][t].shape, got[c][t].dtype)
                if c in (low, high):
                    rim[c - low, t] = jnp.zeros(rim.shape[2:], rim.dtype)

    def w_copy(step):
        peer = peers[step]
        return pltpu.make_async_remote_copy(
            src_ref=w_ref.at[:, pl.ds(pl.multiple_of(peer * out_cols, LANES), out_cols)],
            dst_ref=w_all.at[head],
            send_sem=w_send.at[step],
            recv_sem=w_recv.at[step],
            device_id=(seq, peer),
            device_id_type=MESH,
        )

    for step in range(n_head - 1):
        w_copy(step).start()

    lane = lax.broadcasted_iota(jnp.int32, (bar_len, LANES), 1)
    scaling = HD ** -0.5
    q_load.wait()
    for b in range(bar_count):
        query = replaced(q_ref[b], 0, flag(b)) * scaling
        for t in range(tiles):
            part = query[:, t * LANES : (t + 1) * LANES]
            for h in range(per_tile):
                qs[b, t, h * bar_len : (h + 1) * bar_len, :] = jnp.where(
                    lane // HD == h, part, 0.0
                ).astype(jnp.bfloat16)

    def update(b, t, blocks, first=False, last=False):
        k_at, v_at = slice(0, LANES), slice(LANES, 2 * LANES)
        query = qs[b, t]
        scores = []
        for ref, index, usable in blocks:
            s = lax.dot_general(
                query, ref[index + (slice(None), k_at)], (((1,), (1,)), ((), ())),
                preferred_element_type=jnp.float32,
            )
            if usable is not None:
                s = s + jnp.where(usable, 0.0, NEG).astype(jnp.float32)
            scores.append(s)
        wide = functools.reduce(jnp.maximum, scores)
        peak = jnp.max(wide, axis=1, keepdims=True)
        if not first:
            old = top[b, t][:, :1]
            peak = jnp.maximum(peak, old)
            fade = jnp.exp(old - peak)
        raised = [jnp.exp(s - peak) for s in scores]
        total = jnp.sum(functools.reduce(jnp.add, raised), axis=1, keepdims=True)
        rounded = jnp.concatenate([r.astype(jnp.bfloat16) for r in raised], axis=1)
        value = jnp.concatenate([ref[index + (slice(None), v_at)] for ref, index, _ in blocks], axis=0)
        weighted = jnp.dot(rounded, value, preferred_element_type=jnp.float32)
        if not first:
            total = total + tot[b, t][:, :1] * fade
            weighted = weighted + acc[b, t] * fade
        if not last:
            top[b, t] = jnp.broadcast_to(peak, top.shape[2:])
            tot[b, t] = jnp.broadcast_to(total, tot.shape[2:])
            acc[b, t] = weighted
            return None
        done = weighted / total
        result = done[:bar_len]
        for h in range(1, per_tile):
            result = jnp.where(lane // HD == h, done[h * bar_len : (h + 1) * bar_len], result)
        return result.astype(jnp.bfloat16)

    for t in range(tiles):
        for b in range(bar_count):
            blocks = [(kv, (t, n), None) for n in range(max(b - 1, 0), min(b + 2, bar_count))]
            update(b, t, blocks, first=True)

    def listed_block(b, c, t):
        wanted = listed[b][c]
        slot = jnp.int32(0)
        for other in range(bar_count):
            held = listed[other][c]
            slot = slot + jnp.logical_and(held >= 0, held < wanted).astype(jnp.int32)
        return (got[c][t], (jnp.minimum(slot, CAP - 1),), wanted >= 0)

    twin = head + 1 - 2 * lax.rem(head, 2)
    across = lax.rem(head + 2, n_head)
    chunks = bar_count // CHUNK

    def att_copy(t, g, kind):
        slot = across if kind == 2 else head
        part = att.at[slot, t, g * CHUNK : (g + 1) * CHUNK]
        return pltpu.make_async_remote_copy(
            src_ref=part,
            dst_ref=part,
            send_sem=att_send.at[t, g, kind],
            recv_sem=att_recv.at[t, g, kind],
            device_id=(seq, across if kind == 1 else twin),
            device_id_type=MESH,
        )

    def relay(t, g):
        att_copy(t, g, 1).wait_recv()
        att_copy(t, g, 2).start()

    for t in range(tiles):
        for c in far:

            @pl.when(there(offsets[c]))
            def _(c=c, t=t):
                halo(columns - 1 - c, t).wait_recv()

        for b in range(bar_count):
            update(b, t, [listed_block(b, c, t) for c in far])
        if t > 0:
            for g in range(chunks):
                relay(t - 1, g)
        for c in (low, high):

            @pl.when(there(offsets[c]))
            def _(c=c, t=t):
                halo(columns - 1 - c, t).wait_recv()
                edge(high - c, t).wait_recv()

        for g in range(chunks):
            for b in range(g * CHUNK, (g + 1) * CHUNK):
                blocks = [listed_block(b, c, t) for c in (low, high)]
                if b == 0:
                    blocks.append((rim, (0, t), there(-1)))
                if b == bar_count - 1:
                    blocks.append((rim, (1, t), there(1)))
                att[head, t, b] = update(b, t, blocks, last=True)
            att_copy(t, g, 1).start()
            att_copy(t, g, 0).start()

    own_w.wait()
    for step in range(n_head - 1):
        w_copy(step).wait_recv()
    for g in range(chunks):
        relay(tiles - 1, g)
    for g in range(chunks):
        for t in range(tiles):
            att_copy(t, g, 0).wait_recv()
            att_copy(t, g, 2).wait_recv()
        for b in range(g * CHUNK, (g + 1) * CHUNK):
            summed = None
            for member in range(n_head):
                lhs = jnp.concatenate([att[member, t, b] for t in range(tiles)], axis=1)
                term = jnp.dot(lhs, w_all[member], preferred_element_type=jnp.float32)
                term = term.astype(jnp.bfloat16).astype(jnp.float32)
                summed = term if summed is None else summed + term
            out_ref[b] = summed.astype(jnp.bfloat16)

    for t in range(tiles):
        for c in range(columns):

            @pl.when(there(offsets[c]))
            def _(c=c, t=t):
                halo(c, t).wait_send()
                if c in (low, high):
                    edge(c - low, t).wait_send()

        for g in range(chunks):
            for kind in range(3):
                att_copy(t, g, kind).wait_send()
    for step in range(n_head - 1):
        w_copy(step).wait_send()


def solution(mesh):
    n_seq, n_head = mesh.shape["seq"], mesh.shape["head"]

    def on_device(queries, keys, values, masked, mask_qkv, key_bars, w_out):
        tokens, width = queries.shape
        bars = key_bars.shape[0]
        length = tokens // bars
        cols = w_out.shape[1] // n_head
        tiles, rows = width // LANES, LANES // HD * length
        shaped = [x.reshape(bars, length, width) for x in (queries, keys, values)]
        vmem = pl.BlockSpec(memory_space=pltpu.VMEM)
        dma = pltpu.SemaphoreType.DMA
        out = pl.pallas_call(
            functools.partial(kernel, n_seq, n_head),
            out_shape=jax.ShapeDtypeStruct((bars, length, cols), jnp.bfloat16),
            in_specs=[pl.BlockSpec(memory_space=pltpu.SMEM)] + [vmem] * 2 + [pl.BlockSpec(memory_space=pl.ANY)] * 4,
            out_specs=vmem,
            scratch_shapes=[pltpu.VMEM((bars, length, width), jnp.bfloat16)] * 3
            + [
                dma((3, bars)),
                pltpu.VMEM((tiles, bars, length, 2 * LANES), jnp.bfloat16),
                pltpu.VMEM((bars, tiles, rows, LANES), jnp.bfloat16),
                pltpu.VMEM((2 * R, tiles, CAP, length, 2 * LANES), jnp.bfloat16),
                [pltpu.VMEM((CAP, length, 2 * LANES), jnp.bfloat16)] * (2 * R * tiles),
                pltpu.VMEM((2, tiles, length, 2 * LANES), jnp.bfloat16),
                pltpu.VMEM((n_head, width, cols), jnp.bfloat16),
                pltpu.VMEM((n_head, tiles, bars, length, LANES), jnp.bfloat16),
                pltpu.VMEM((bars, tiles, rows, LANES), jnp.float32),
                pltpu.VMEM((bars, tiles, rows, LANES), jnp.float32),
                pltpu.VMEM((bars, tiles, rows, LANES), jnp.float32),
                dma((2 * R, tiles)),
                dma((2 * R, tiles)),
                dma((2, tiles)),
                dma((2, tiles)),
                dma((n_head - 1,)),
                dma((n_head - 1,)),
                dma,
                dma((tiles, bars // CHUNK, 3)),
                dma((tiles, bars // CHUNK, 3)),
            ],
            compiler_params=pltpu.CompilerParams(
                collective_id=0, has_side_effects=True
            ),
            name="bar_attention",
        )(key_bars, masked.reshape(bars, length), mask_qkv, *shaped, w_out)
        return out.reshape(tokens, cols)

    placed = (
        P("seq", "head"),
        P("seq", "head"),
        P("seq", "head"),
        P("seq"),
        P(None, "head"),
        P("seq", None),
        P("head", None),
    )
    return jax.shard_map(
        on_device, mesh=mesh, in_specs=placed, out_specs=P("seq", "head"), check_vma=False
    )
```

```python
import functools

import jax
import jax.numpy as jnp
from jax import lax
from jax.experimental import pallas as pl
from jax.experimental.pallas import tpu as pltpu
from jax.sharding import PartitionSpec as P

HD = 64
R = 2
CAP = 2
CHUNK = 1
LANES = 128
MESH = pl.DeviceIdType.MESH
NEG = -1e30


def kernel(
    n_seq, n_head, bars_hbm, masked_hbm, mask_hbm, q_hbm, k_hbm, v_hbm, w_ref, out_ref,
    bars_ref, masked_ref, mask_ref, small_sem, q_ref, k_ref, v_ref, in_sem,    kv, qs, pack, got_refs, rim, w_all, att, top, tot, acc,
    halo_send, halo_recv, rim_send, rim_recv, w_send, w_recv, w_own, att_send, att_recv,
):
    seq = lax.axis_index("seq")
    head = lax.axis_index("head")
    bar_count, bar_len, width = q_ref.shape
    tiles = width // LANES
    per_tile = LANES // HD
    out_cols = w_all.shape[2]
    columns = 2 * R
    got = [got_refs[c * tiles : (c + 1) * tiles] for c in range(columns)]
    offsets = [c - R if c < R else c - R + 1 for c in range(columns)]
    low, high = R - 1, R

    def there(offset):
        return jnp.logical_and(seq + offset >= 0, seq + offset < n_seq)

    barrier = pltpu.get_barrier_semaphore()
    count = n_head - 1
    for offset in offsets:
        count = count + there(offset).astype(jnp.int32)

        @pl.when(there(offset))
        def _(offset=offset):
            pl.semaphore_signal(
                barrier, inc=1, device_id=(seq + offset, head), device_id_type=MESH
            )

    peers = [lax.rem(head + step, n_head) for step in range(1, n_head)]
    for peer in peers:
        pl.semaphore_signal(barrier, inc=1, device_id=(seq, peer), device_id_type=MESH)

    small = [
        pltpu.make_async_copy(source, target, small_sem.at[n])
        for n, (source, target) in enumerate(
            ((masked_hbm, masked_ref), (mask_hbm, mask_ref), (bars_hbm, bars_ref))
        )
    ]
    for load in small:
        load.start()
    bar_order = [bar_count - 1, 0] + list(range(1, bar_count - 1))
    loads = {}
    for n, (source, target) in enumerate(((k_hbm, k_ref), (v_hbm, v_ref))):
        for b in range(bar_count):
            loads[n, b] = pltpu.make_async_copy(source.at[b], target.at[b], in_sem.at[n, b])
    for b in bar_order:
        loads[0, b].start()
        loads[1, b].start()
    q_load = pltpu.make_async_copy(q_hbm, q_ref, in_sem.at[2, 0])
    q_load.start()
    own_w = pltpu.make_async_copy(
        w_ref.at[:, pl.ds(pl.multiple_of(head * out_cols, LANES), out_cols)],
        w_all.at[head],
        w_own,
    )
    own_w.start()

    rows = lax.broadcasted_iota(jnp.int32, (bar_len, bar_len), 0)
    cols = lax.broadcasted_iota(jnp.int32, (bar_len, bar_len), 1)

    def flag(b):
        row = masked_ref[b : b + 1, :]
        return jnp.max(jnp.where(rows == cols, row, 0), axis=1, keepdims=True) == 1

    def replaced(value, row, hit):
        return jnp.where(hit, mask_ref[row : row + 1, :].astype(jnp.float32), value.astype(jnp.float32))

    def prepare(b):
        loads[0, b].wait()
        loads[1, b].wait()
        hit = flag(b)
        key_eff = replaced(k_ref[b], 1, hit).astype(jnp.bfloat16)
        value_eff = replaced(v_ref[b], 2, hit).astype(jnp.bfloat16)
        for t in range(tiles):
            kv[t, b, :, :LANES] = key_eff[:, t * LANES : (t + 1) * LANES]
            kv[t, b, :, LANES:] = value_eff[:, t * LANES : (t + 1) * LANES]

    for load in small:
        load.wait()
    for b in bar_order[:2]:
        prepare(b)

    listed = [[bars_ref[b, c] for c in range(columns)] for b in range(bar_count)]
    picks = []
    for c in range(columns):
        before = jnp.int32(0)
        chosen = [jnp.int32(0)] * CAP
        for b in range(bar_count):
            used = (listed[b][c] >= 0).astype(jnp.int32)
            for slot in range(CAP):
                chosen[slot] = chosen[slot] + jnp.where(before == slot, used * b, 0)
            before = before + used
        picks.append(chosen)

    pl.semaphore_wait(barrier, count)

    def halo(c, t):
        return pltpu.make_async_remote_copy(
            src_ref=pack.at[c, t],
            dst_ref=got[columns - 1 - c][t],
            send_sem=halo_send.at[c, t],
            recv_sem=halo_recv.at[columns - 1 - c, t],
            device_id=(seq + offsets[c], head),
            device_id_type=MESH,
        )

    def edge(side, t):
        return pltpu.make_async_remote_copy(
            src_ref=kv.at[t, bar_count - 1 if side else 0],
            dst_ref=rim.at[1 - side, t],
            send_sem=rim_send.at[side, t],
            recv_sem=rim_recv.at[1 - side, t],
            device_id=(seq + (1 if side else -1), head),
            device_id_type=MESH,
        )

    far = [c for c in range(columns) if c not in (low, high)]
    for c in (low, high):

        @pl.when(there(offsets[c]))
        def _(c=c):
            edge(c - low, 0).start()

    for b in bar_order[2:]:
        prepare(b)
    stages = [(t, c) for group in (far, (low, high)) for t in range(tiles) for c in group]
    for t, c in stages:
        for slot in range(CAP):
            pack[c, t, slot] = kv[t, picks[c][slot]]

        @pl.when(there(offsets[c]))
        def _(c=c, t=t):
            if c in (low, high) and t > 0:
                edge(c - low, t).start()
            halo(c, t).start()

        @pl.when(jnp.logical_not(there(offsets[c])))
        def _(c=c, t=t):
            got[c][t][...] = jnp.zeros(got[c][t].shape, got[c][t].dtype)
            if c in (low, high):
                rim[c - low, t] = jnp.zeros(rim.shape[2:], rim.dtype)

    def w_copy(step):
        peer = peers[step]
        return pltpu.make_async_remote_copy(
            src_ref=w_ref.at[:, pl.ds(pl.multiple_of(peer * out_cols, LANES), out_cols)],
            dst_ref=w_all.at[head],
            send_sem=w_send.at[step],
            recv_sem=w_recv.at[step],
            device_id=(seq, peer),
            device_id_type=MESH,
        )

    for step in range(n_head - 1):
        w_copy(step).start()

    lane = lax.broadcasted_iota(jnp.int32, (bar_len, LANES), 1)
    scaling = HD ** -0.5
    q_load.wait()
    for b in range(bar_count):
        query = replaced(q_ref[b], 0, flag(b)) * scaling
        for t in range(tiles):
            part = query[:, t * LANES : (t + 1) * LANES]
            for h in range(per_tile):
                qs[b, t, h * bar_len : (h + 1) * bar_len, :] = jnp.where(
                    lane // HD == h, part, 0.0
                ).astype(jnp.bfloat16)

    def update(b, t, blocks, first=False, last=False):
        k_at, v_at = slice(0, LANES), slice(LANES, 2 * LANES)
        query = qs[b, t]
        scores = []
        for ref, index, usable in blocks:
            s = lax.dot_general(
                query, ref[index + (slice(None), k_at)], (((1,), (1,)), ((), ())),
                preferred_element_type=jnp.float32,
            )
            if usable is not None:
                s = s + jnp.where(usable, 0.0, NEG).astype(jnp.float32)
            scores.append(s)
        wide = functools.reduce(jnp.maximum, scores)
        peak = jnp.max(wide, axis=1, keepdims=True)
        if not first:
            old = top[b, t][:, :1]
            peak = jnp.maximum(peak, old)
            fade = jnp.exp(old - peak)
        raised = [jnp.exp(s - peak) for s in scores]
        total = jnp.sum(functools.reduce(jnp.add, raised), axis=1, keepdims=True)
        rounded = jnp.concatenate([r.astype(jnp.bfloat16) for r in raised], axis=1)
        value = jnp.concatenate([ref[index + (slice(None), v_at)] for ref, index, _ in blocks], axis=0)
        weighted = jnp.dot(rounded, value, preferred_element_type=jnp.float32)
        if not first:
            total = total + tot[b, t][:, :1] * fade
            weighted = weighted + acc[b, t] * fade
        if not last:
            top[b, t] = jnp.broadcast_to(peak, top.shape[2:])
            tot[b, t] = jnp.broadcast_to(total, tot.shape[2:])
            acc[b, t] = weighted
            return None
        done = weighted / total
        result = done[:bar_len]
        for h in range(1, per_tile):
            result = jnp.where(lane // HD == h, done[h * bar_len : (h + 1) * bar_len], result)
        return result.astype(jnp.bfloat16)

    for t in range(tiles):
        for b in range(bar_count):
            blocks = [(kv, (t, n), None) for n in range(max(b - 1, 0), min(b + 2, bar_count))]
            update(b, t, blocks, first=True)

    def listed_block(b, c, t):
        wanted = listed[b][c]
        slot = jnp.int32(0)
        for other in range(bar_count):
            held = listed[other][c]
            slot = slot + jnp.logical_and(held >= 0, held < wanted).astype(jnp.int32)
        return (got[c][t], (jnp.minimum(slot, CAP - 1),), wanted >= 0)

    twin = head + 1 - 2 * lax.rem(head, 2)
    across = lax.rem(head + 2, n_head)
    chunks = bar_count // CHUNK

    def att_copy(t, g, kind):
        slot = across if kind == 2 else head
        part = att.at[slot, t, g * CHUNK : (g + 1) * CHUNK]
        return pltpu.make_async_remote_copy(
            src_ref=part,
            dst_ref=part,
            send_sem=att_send.at[t, g, kind],
            recv_sem=att_recv.at[t, g, kind],
            device_id=(seq, across if kind == 1 else twin),
            device_id_type=MESH,
        )

    def relay(t, g):
        att_copy(t, g, 1).wait_recv()
        att_copy(t, g, 2).start()

    for t in range(tiles):
        for c in far:

            @pl.when(there(offsets[c]))
            def _(c=c, t=t):
                halo(columns - 1 - c, t).wait_recv()

        for b in range(bar_count):
            update(b, t, [listed_block(b, c, t) for c in far])
        if t > 0:
            for g in range(chunks):
                relay(t - 1, g)
        for c in (low, high):

            @pl.when(there(offsets[c]))
            def _(c=c, t=t):
                halo(columns - 1 - c, t).wait_recv()
                edge(high - c, t).wait_recv()

        for g in range(chunks):
            for b in range(g * CHUNK, (g + 1) * CHUNK):
                blocks = [listed_block(b, c, t) for c in (low, high)]
                if b == 0:
                    blocks.append((rim, (0, t), there(-1)))
                if b == bar_count - 1:
                    blocks.append((rim, (1, t), there(1)))
                att[head, t, b] = update(b, t, blocks, last=True)
            att_copy(t, g, 1).start()
            att_copy(t, g, 0).start()

    own_w.wait()
    for step in range(n_head - 1):
        w_copy(step).wait_recv()
    for g in range(chunks):
        relay(tiles - 1, g)
    for g in range(chunks):
        for t in range(tiles):
            att_copy(t, g, 0).wait_recv()
            att_copy(t, g, 2).wait_recv()
        for b in range(g * CHUNK, (g + 1) * CHUNK):
            summed = None
            for member in range(n_head):
                lhs = jnp.concatenate([att[member, t, b] for t in range(tiles)], axis=1)
                term = jnp.dot(lhs, w_all[member], preferred_element_type=jnp.float32)
                term = term.astype(jnp.bfloat16).astype(jnp.float32)
                summed = term if summed is None else summed + term
            out_ref[b] = summed.astype(jnp.bfloat16)

    for t in range(tiles):
        for c in range(columns):

            @pl.when(there(offsets[c]))
            def _(c=c, t=t):
                halo(c, t).wait_send()
                if c in (low, high):
                    edge(c - low, t).wait_send()

        for g in range(chunks):
            for kind in range(3):
                att_copy(t, g, kind).wait_send()
    for step in range(n_head - 1):
        w_copy(step).wait_send()


def solution(mesh):
    n_seq, n_head = mesh.shape["seq"], mesh.shape["head"]

    def on_device(queries, keys, values, masked, mask_qkv, key_bars, w_out):
        tokens, width = queries.shape
        bars = key_bars.shape[0]
        length = tokens // bars
        cols = w_out.shape[1] // n_head
        tiles, rows = width // LANES, LANES // HD * length
        shaped = [x.reshape(bars, length, width) for x in (queries, keys, values)]
        vmem = pl.BlockSpec(memory_space=pltpu.VMEM)
        dma = pltpu.SemaphoreType.DMA
        out = pl.pallas_call(
            functools.partial(kernel, n_seq, n_head),
            out_shape=jax.ShapeDtypeStruct((bars, length, cols), jnp.bfloat16),
            in_specs=[pl.BlockSpec(memory_space=pl.ANY)] * 7,
            out_specs=vmem,
            scratch_shapes=[
                pltpu.SMEM(key_bars.shape, jnp.int32),
                pltpu.VMEM((bars, length), jnp.int32),
                pltpu.VMEM(mask_qkv.shape, jnp.bfloat16),
                dma((3,)),
            ]
            + [pltpu.VMEM((bars, length, width), jnp.bfloat16)] * 3
            + [
                dma((3, bars)),
                pltpu.VMEM((tiles, bars, length, 2 * LANES), jnp.bfloat16),
                pltpu.VMEM((bars, tiles, rows, LANES), jnp.bfloat16),
                pltpu.VMEM((2 * R, tiles, CAP, length, 2 * LANES), jnp.bfloat16),
                [pltpu.VMEM((CAP, length, 2 * LANES), jnp.bfloat16)] * (2 * R * tiles),
                pltpu.VMEM((2, tiles, length, 2 * LANES), jnp.bfloat16),
                pltpu.VMEM((n_head, width, cols), jnp.bfloat16),
                pltpu.VMEM((n_head, tiles, bars, length, LANES), jnp.bfloat16),
                pltpu.VMEM((bars, tiles, rows, LANES), jnp.float32),
                pltpu.VMEM((bars, tiles, rows, LANES), jnp.float32),
                pltpu.VMEM((bars, tiles, rows, LANES), jnp.float32),
                dma((2 * R, tiles)),
                dma((2 * R, tiles)),
                dma((2, tiles)),
                dma((2, tiles)),
                dma((n_head - 1,)),
                dma((n_head - 1,)),
                dma,
                dma((tiles, bars // CHUNK, 3)),
                dma((tiles, bars // CHUNK, 3)),
            ],
            compiler_params=pltpu.CompilerParams(
                collective_id=0, has_side_effects=True
            ),
            name="bar_attention",
        )(key_bars, masked.reshape(bars, length), mask_qkv, *shaped, w_out)
        return out.reshape(tokens, cols)

    placed = (
        P("seq", "head"),
        P("seq", "head"),
        P("seq", "head"),
        P("seq"),
        P(None, "head"),
        P("seq", None),
        P("head", None),
    )
    return jax.shard_map(
        on_device, mesh=mesh, in_specs=placed, out_specs=P("seq", "head"), check_vma=False
    )
```
